512 devices in a mesh: rows: 64 (over x, z, core), cols: 8 (over y).
Axes of the slice: x: 4, y: 8, z: 8, core: 2. Of those that a mesh axis runs over, the one named last changes fastest.
Arguments:
- right_sides: float32 [4, 64, 128, 256], P(None, 'rows'), may hold values from -6 to 6
- factor_blocks: bfloat16 [3, 64, 8, 8, 256, 256], P(None, 'rows', 'cols'), may hold values from -0.125 to 0.125
- diag_inverses: bfloat16 [4, 64, 256, 256], P(None, 'rows')
- source_ids: int32 [3, 64, 8, 8], P(None, 'rows', 'cols'), may hold values from 0 to 191, as said below
- block_counts: int32 [3, 64, 8], P(None, 'rows', 'cols'), may hold values from 1 to 8, as said below
Outputs:
- solution: float32 [4, 64, 128, 256], P(None, 'rows', 'cols')
The draws below stay inside these ranges and needn't reach their ends.
Inputs may be any that keep to these rules, and one draw needn't show every extreme that they name: source_ids[l, t, c, k] = m * 64 + s names a supernode of a level m <= l with s % 8 == c. block_counts[l, t, c] slots of target t on group c hold blocks of the factor; slots at and past it are not part of the factor. In every level some target and group has all 8 slots live.
All inputs are finite; a program needn't handle non-finite values.
Results may differ from the reference program's by a relative error of at most 0.007.
Values may be sent and summed in bfloat16 or wider, within the bound.
A program may use at most 128 MiB of HBM per device.

```python
import math
import jax
import jax.numpy as jnp
from jax import lax

W = 256
RHS = 128
LEV = 4
BPD = 8
SUPER = 64
COLGRP = 8


def draw_diag_inverses(key, part):
    first_key, second_key = jax.random.split(key)
    diagonal = jax.random.uniform(first_key, (LEV, SUPER, W), jnp.float32, 0.6, 1.4)
    spread = jax.random.normal(second_key, (LEV, SUPER, W, W), jnp.float32) * (0.5 / math.sqrt(W))
    identity = jnp.eye(W, dtype=jnp.float32)
    return (spread + identity * diagonal[..., None, :]).astype(jnp.bfloat16)


def draw_source_ids(key, part):
    first_key, second_key = jax.random.split(key)
    shape = (LEV - 1, SUPER, COLGRP, BPD)
    ceiling = (jnp.arange(LEV - 1, dtype=jnp.int32) + 1).reshape(LEV - 1, 1, 1, 1)
    source_level = jax.random.randint(first_key, shape, 0, 12 * LEV, dtype=jnp.int32) % ceiling
    quotient = jax.random.randint(second_key, shape, 0, SUPER // COLGRP, dtype=jnp.int32)
    column = jnp.arange(COLGRP, dtype=jnp.int32).reshape(1, 1, COLGRP, 1)
    chosen = source_level * SUPER + quotient * COLGRP + column
    chosen = chosen.at[0, 0, 0, 0].set(0)
    chosen = chosen.at[LEV - 2, 0, COLGRP - 1, 0].set((LEV - 1) * SUPER - 1)
    return chosen


def draw_block_counts(key, part):
    first_key, second_key, third_key = jax.random.split(key, 3)
    shape = (LEV - 1, SUPER, COLGRP)
    raw_draws = jax.random.randint(first_key, shape, 0, BPD, dtype=jnp.int32)
    counted = 1 + raw_draws * raw_draws // max(BPD - 1, 1)
    places = SUPER * COLGRP
    position = jnp.arange(places, dtype=jnp.int32).reshape(1, SUPER, COLGRP)
    busiest = jax.random.randint(second_key, (LEV - 1, 1, 1), 0, places, dtype=jnp.int32)
    lightest = (busiest + 1 + jax.random.randint(third_key, (LEV - 1, 1, 1), 0, places - 1, dtype=jnp.int32)) % places
    counted = jnp.where(position == busiest, BPD, counted)
    counted = jnp.where(position == lightest, 1, counted)
    return counted.astype(jnp.int32)


def levels(stream_key, shape, pieces, low, top_value):
    factor_of, own = 1.0, jax.random.fold_in(stream_key, 6)
    for dim, parts in pieces:
        steps = jnp.exp(jax.random.uniform(jax.random.fold_in(own, dim), (parts,), jnp.float32, low / len(pieces), top_value / len(pieces)))
        factor_of = factor_of * jnp.repeat(steps, shape[dim] // parts).reshape([-1 if axis == dim else 1 for axis in range(len(shape))])
    return factor_of


def scatter_about(rng, extent, scale, most, pieces=(), kind=jnp.bfloat16):
    entries = jax.random.normal(rng, extent, jnp.float32) * scale
    if len(pieces) > 0:
        entries = levels(rng, extent, pieces, -0.22, 0.18) * entries
    return jnp.clip(entries, min=-most, max=most).astype(kind)


def setup_inputs(seed: int = 0) -> dict:
    keys = jax.random.split(jax.random.key(seed), 6)
    return {
        "right_sides": scatter_about(keys[0], (LEV, SUPER, RHS, W), 1.0, 6.0, ((1, 64),), jnp.float32),
        "factor_blocks": scatter_about(keys[1], (LEV - 1, SUPER, COLGRP, BPD, W, W), (W * BPD) ** -0.5, 0.125, ((1, 64), (2, 8))),
        "diag_inverses": draw_diag_inverses(jax.random.fold_in(keys[5], 71), 0),
        "source_ids": draw_source_ids(jax.random.fold_in(keys[5], 71), 0),
        "block_counts": draw_block_counts(jax.random.fold_in(keys[5], 71), 0),
    }


def reference(right_sides, factor_blocks, diag_inverses, source_ids, block_counts):
    solved = jnp.zeros((LEV * SUPER, RHS, W), jnp.bfloat16)
    slot_range = jnp.arange(BPD, dtype=jnp.int32)
    solutions = []
    for level_index in range(LEV):
        if level_index == 0:
            update = jnp.zeros((SUPER, RHS, W), jnp.float32)
        else:
            current_store = solved

            def one_target(items):
                blocks, chosen_ids, live_counts = items
                inputs = current_store[chosen_ids].astype(jnp.float32)
                live_mask = (slot_range[None, :] < live_counts[:, None]).astype(jnp.float32)
                return jnp.einsum("ckaw,ckwb,ck->ab", inputs, blocks.astype(jnp.float32), live_mask)

            update = lax.map(one_target, (factor_blocks[level_index - 1], source_ids[level_index - 1], block_counts[level_index - 1]))
        reduced = (right_sides[level_index] - update).astype(jnp.bfloat16)
        solution = jnp.einsum("saw,swb->sab", reduced.astype(jnp.float32), diag_inverses[level_index].astype(jnp.float32))
        solutions.append(solution)
        solved = solved.at[level_index * SUPER:(level_index + 1) * SUPER].set(solution.astype(jnp.bfloat16))
    return jnp.stack(solutions)
```

```python
import jax
import jax.numpy as jnp
from jax import lax
from jax.experimental import pallas as pl
from jax.experimental.pallas import tpu as pltpu
from jax.sharding import PartitionSpec as P

LEV, NX, NZ, NC, NY = 4, 4, 8, 2, 8
W, RHS, BPD = 256, 128, 8
SHARE = RHS // NY
FAR8 = (4, 3, 5, 2, 6, 1, 7)
FAR4 = (2, 1, 3)
MESH = pl.DeviceIdType.MESH


def kernel(
    ids_ref, counts_ref, rhs_hbm, fac_hbm, diag_hbm, out_ref,
    store0, store1, store2, part, landed, rhs_full, rhs_own, fac, diag, piece,
    load_sem, r_send, r_recv, a_send, a_recv, b_send, b_recv, c_send, c_recv, d_send, d_recv,
):
    stores = (store0, store1, store2)
    row = lax.axis_index("rows")
    col = lax.axis_index("cols")
    x = row // (NZ * NC)
    z = (row // NC) % NZ
    core = row % NC
    root = row % NY
    src_core = col % NC
    in_lane = core == src_core
    is_root = root == col
    own_half = z // (NZ // 2)
    own_slot = 2 * x + own_half

    def rows_of(xx, zz, cc):
        return (xx * NZ + zz) * NC + cc

    own_rows = pl.ds(pl.multiple_of(col * SHARE, SHARE), SHARE)

    loads = [
        pltpu.make_async_copy(rhs_hbm.at[0, 0], rhs_full, load_sem.at[0]),
        pltpu.make_async_copy(diag_hbm.at[0, 0], diag.at[0], load_sem.at[1]),
        pltpu.make_async_copy(rhs_hbm.at[:, 0, own_rows, :], rhs_own, load_sem.at[2]),
    ]
    for level in range(1, LEV):
        loads.append(
            pltpu.make_async_copy(fac_hbm.at[level - 1, 0, 0], fac.at[level - 1], load_sem.at[1 + 2 * level])
        )
        loads.append(pltpu.make_async_copy(diag_hbm.at[level, 0], diag.at[level], load_sem.at[2 + 2 * level]))
    for copy in loads:
        copy.start()

    barrier = pltpu.get_barrier_semaphore()
    for d in FAR8:
        pl.semaphore_signal(barrier, device_id=(row, (col + d) % NY), device_id_type=MESH)
        pl.semaphore_signal(barrier, device_id=(rows_of(x, (z + d) % NZ, core), col), device_id_type=MESH)
    for d in FAR4:
        pl.semaphore_signal(barrier, device_id=(rows_of((x + d) % NX, z, core), col), device_id_type=MESH)
    pl.semaphore_signal(barrier, device_id=(rows_of(x, z, 1 - core), col), device_id_type=MESH)

    def r_copy(level, d):
        to = (col + d) % NY
        return pltpu.make_async_remote_copy(
            part.at[level - 1, pl.ds(pl.multiple_of(to * SHARE, SHARE), SHARE), :],
            landed.at[level - 1, d],
            r_send.at[level - 1, d],
            r_recv.at[level - 1, d],
            device_id=(row, to),
            device_id_type=MESH,
        )

    def a_copy(level):
        return pltpu.make_async_remote_copy(
            piece.at[level - 1],
            stores[level].at[own_slot, own_rows, :],
            a_send.at[level - 1],
            a_recv.at[level - 1, col],
            device_id=(row, root),
            device_id_type=MESH,
        )

    def a_wait(level, d):
        frm = (col + d) % NY
        pltpu.make_async_remote_copy(
            piece.at[level - 1],
            stores[level].at[own_slot, pl.ds(pl.multiple_of(frm * SHARE, SHARE), SHARE), :],
            a_send.at[level - 1],
            a_recv.at[level - 1, frm],
            device_id=(row, frm),
            device_id_type=MESH,
        ).wait_recv()

    def b_copy(level, half, d):
        slot = 2 * x + half
        return pltpu.make_async_remote_copy(
            stores[level].at[slot],
            stores[level].at[slot],
            b_send.at[level, d],
            b_recv.at[level, half],
            device_id=(rows_of(x, (z + d) % NZ, core), col),
            device_id_type=MESH,
        )

    def c_copy(level, from_x, half, d):
        slot = 2 * from_x + half
        return pltpu.make_async_remote_copy(
            stores[level].at[slot],
            stores[level].at[slot],
            c_send.at[level, d, half],
            c_recv.at[level, d, half],
            device_id=(rows_of((x + d) % NX, z, core), col),
            device_id_type=MESH,
        )

    def d_copy(level, slot):
        return pltpu.make_async_remote_copy(
            stores[level].at[slot],
            stores[level].at[slot],
            d_send.at[level, slot],
            d_recv.at[level, slot],
            device_id=(rows_of(x, z, 1 - core), col),
            device_id_type=MESH,
        )

    def relay(level, half):
        for d in FAR4:
            c_copy(level, x, half, d).start()
        d_copy(level, 2 * x + half).start()

    def spread(level):
        @pl.when(is_root)
        def _():
            if level > 0:
                for d in range(1, NY):
                    a_wait(level, d)
            for d in FAR8:
                b_copy(level, own_half, d).start()
            relay(level, own_half)

        @pl.when(in_lane)
        def _():
            for other in range(2):
                half = (own_half + 1 + other) % 2

                @pl.when(jnp.logical_not(jnp.logical_and(is_root, half == own_half)))
                def _():
                    b_copy(level, half, 1).wait_recv()
                    relay(level, half)

            for d in (1, 3, 2):
                from_x = (x + NX - d) % NX
                for half in range(2):
                    c_copy(level, from_x, half, d).wait_recv()
                    d_copy(level, 2 * from_x + half).start()

        @pl.when(jnp.logical_not(in_lane))
        def _():
            for slot in range(8):
                d_copy(level, slot).wait_recv()

    def drain(level):
        if level > 0:
            for d in FAR8:
                r_copy(level, d).wait_send()
        if level == LEV - 1:
            return
        if level > 0:

            @pl.when(jnp.logical_not(is_root))
            def _():
                a_copy(level).wait_send()

        @pl.when(is_root)
        def _():
            for d in FAR8:
                b_copy(level, own_half, d).wait_send()

        @pl.when(in_lane)
        def _():
            for half in range(2):
                for d in FAR4:
                    c_copy(level, x, half, d).wait_send()
            for slot in range(8):
                d_copy(level, slot).wait_send()

    loads[0].wait()
    loads[1].wait()

    @pl.when(is_root)
    def _():
        whole = jnp.dot(rhs_full[...].astype(jnp.bfloat16), diag[0], preferred_element_type=jnp.float32)
        store0[own_slot] = whole.astype(jnp.bfloat16)

    pl.semaphore_wait(barrier, 2 * (NY - 1) + NX)
    loads[2].wait()
    out_ref[0] = jnp.dot(rhs_own[0].astype(jnp.bfloat16), diag[0], preferred_element_type=jnp.float32)
    spread(0)

    for level in range(1, LEV):
        loads[1 + 2 * level].wait()
        loads[2 + 2 * level].wait()
        live = counts_ref[level - 1]
        total = jnp.zeros((RHS, W), jnp.float32)
        for k in range(BPD):
            source = ids_ref[(level - 1) * BPD + k]
            place = (source % (NX * NZ * NC)) // NY
            held = source // (NX * NZ * NC)
            block = store0[place]
            for m in range(1, level):
                block = lax.select(held == m, stores[m][place], block)
            block = lax.select(k < live, block, jnp.zeros_like(block))
            total = total + jnp.dot(block, fac[level - 1, k], preferred_element_type=jnp.float32)
        part[level - 1] = total
        for d in FAR8:
            r_copy(level, d).start()
        update = part[level - 1, own_rows, :]
        for d in (1, 7, 2, 6, 3, 5, 4):
            r_copy(level, d).wait_recv()
            update = update + landed[level - 1, d]
        reduced = (rhs_own[level] - update).astype(jnp.bfloat16)
        solved = jnp.dot(reduced, diag[level], preferred_element_type=jnp.float32)
        out_ref[level] = solved
        if level < LEV - 1:

            @pl.when(is_root)
            def _():
                stores[level][own_slot, own_rows, :] = solved.astype(jnp.bfloat16)

            @pl.when(jnp.logical_not(is_root))
            def _():
                piece[level - 1] = solved.astype(jnp.bfloat16)
                a_copy(level).start()

            spread(level)

    for level in range(LEV):
        drain(level)


def shards(right_sides, factor_blocks, diag_inverses, source_ids, block_counts):
    dma = pltpu.SemaphoreType.DMA
    hbm = pl.BlockSpec(memory_space=pl.ANY)
    smem = pl.BlockSpec(memory_space=pltpu.SMEM)
    store = pltpu.VMEM((8, RHS, W), jnp.bfloat16)
    out = pl.pallas_call(
        kernel,
        out_shape=jax.ShapeDtypeStruct((LEV, SHARE, W), jnp.float32),
        in_specs=[smem, smem, hbm, hbm, hbm],
        out_specs=pl.BlockSpec(memory_space=pltpu.VMEM),
        scratch_shapes=[
            store, store, store,
            pltpu.VMEM((LEV - 1, RHS, W), jnp.float32),
            pltpu.VMEM((LEV - 1, NY, SHARE, W), jnp.float32),
            pltpu.VMEM((RHS, W), jnp.float32),
            pltpu.VMEM((LEV, SHARE, W), jnp.float32),
            pltpu.VMEM((LEV - 1, BPD, W, W), jnp.bfloat16),
            pltpu.VMEM((LEV, W, W), jnp.bfloat16),
            pltpu.VMEM((LEV - 2, SHARE, W), jnp.bfloat16),
            dma((3 + 2 * LEV,)),
            dma((LEV - 1, NY)), dma((LEV - 1, NY)),
            dma((LEV - 2,)), dma((LEV - 2, NY)),
            dma((LEV - 1, NZ)), dma((LEV - 1, 2)),
            dma((LEV - 1, NX, 2)), dma((LEV - 1, NX, 2)),
            dma((LEV - 1, 8)), dma((LEV - 1, 8)),
        ],
        compiler_params=pltpu.CompilerParams(collective_id=0, has_side_effects=True),
        name="levels",
    )(
        source_ids.reshape((LEV - 1) * BPD),
        block_counts.reshape(LEV - 1),
        right_sides,
        factor_blocks,
        diag_inverses,
    )
    return out[:, None]


def solution(mesh):
    return jax.shard_map(
        shards,
        mesh=mesh,
        in_specs=(
            P(None, "rows", None, None),
            P(None, "rows", "cols", None, None, None),
            P(None, "rows", None, None),
            P(None, "rows", "cols", None),
            P(None, "rows", "cols"),
        ),
        out_specs=P(None, "rows", "cols", None),
        check_vma=False,
    )
```

```python
import jax
import jax.numpy as jnp
from jax import lax
from jax.experimental import pallas as pl
from jax.experimental.pallas import tpu as pltpu
from jax.sharding import PartitionSpec as P

LEV, NX, NZ, NC, NY = 4, 4, 8, 2, 8
W, RHS, BPD = 256, 128, 8
SHARE = RHS // NY
FAR8 = (4, 3, 5, 2, 6, 1, 7)
FAR4 = (2, 1, 3)
NCH = 1
CHUNK = [pl.ds(i * (RHS // NCH), RHS // NCH) for i in range(NCH)]
MESH = pl.DeviceIdType.MESH


def kernel(
    ids_ref, counts_ref, rhs_hbm, fac_hbm, diag_hbm, out_ref,
    store0, store1, store2, part, part16, landed, last, solbuf, obuf, rhs_full, rhs_own, fac, diag,
    load_sem, r_send, r_recv, l_send, l_recv, o_send, o_recv,
    b_send, b_recv, e_send, e_recv, x_send, x_recv, c_send, c_recv, d_send, d_recv,
):
    stores = (store0, store1, store2)
    row = lax.axis_index("rows")
    col = lax.axis_index("cols")
    x = row // (NZ * NC)
    z = (row // NC) % NZ
    core = row % NC
    root = row % NY
    src_core = col % NC
    in_lane = core == src_core
    is_root = root == col
    not_root = jnp.logical_not(is_root)
    own_half = z // (NZ // 2)
    own_slot = 2 * x + own_half
    across = (x + NX // 2) % NX

    def rows_of(xx, zz, cc):
        return (xx * NZ + zz) * NC + cc

    def share(c):
        return pl.ds(pl.multiple_of(c * SHARE, SHARE), SHARE)

    def send(src, dst, send_sem, recv_sem, r, c):
        return pltpu.make_async_remote_copy(src, dst, send_sem, recv_sem, device_id=(r, c), device_id_type=MESH)

    loads = [
        pltpu.make_async_copy(rhs_hbm.at[0, 0], rhs_full.at[0], load_sem.at[0]),
        pltpu.make_async_copy(diag_hbm.at[0, 0], diag.at[0], load_sem.at[1]),
        pltpu.make_async_copy(rhs_hbm.at[:, 0, share(col), :], rhs_own, load_sem.at[2]),
    ]
    for level in range(1, LEV):
        loads.append(
            pltpu.make_async_copy(fac_hbm.at[level - 1, 0, 0], fac.at[level - 1], load_sem.at[1 + 2 * level])
        )
        loads.append(pltpu.make_async_copy(diag_hbm.at[level, 0], diag.at[level], load_sem.at[2 + 2 * level]))
    for level in range(1, LEV - 1):
        loads.append(
            pltpu.make_async_copy(rhs_hbm.at[level, 0], rhs_full.at[level], load_sem.at[2 + 2 * (LEV - 1) + level])
        )
    for copy in loads:
        copy.start()

    barrier = pltpu.get_barrier_semaphore()
    for d in FAR8:
        pl.semaphore_signal(barrier, device_id=(row, (col + d) % NY), device_id_type=MESH)
        pl.semaphore_signal(barrier, device_id=(rows_of(x, (z + d) % NZ, core), col), device_id_type=MESH)
    for d in FAR4:
        pl.semaphore_signal(barrier, device_id=(rows_of((x + d) % NX, z, core), col), device_id_type=MESH)
    pl.semaphore_signal(barrier, device_id=(rows_of(x, z, 1 - core), col), device_id_type=MESH)

    def l_copy(d):
        to = (col + d) % NY
        return send(part16.at[LEV - 2, share(to), :], last.at[d], l_send.at[d], l_recv.at[d], row, to)

    def r_copy(level, ch, d):
        return send(
            part16.at[level - 1, CHUNK[ch], :],
            landed.at[level - 1, d, CHUNK[ch], :],
            r_send.at[level - 1, ch],
            r_recv.at[level - 1, ch, d],
            row,
            root,
        )

    def o_copy(level, d):
        to = (col + d) % NY
        return send(
            solbuf.at[level - 1, share(to), :], obuf.at[level - 1], o_send.at[level - 1, d], o_recv.at[level - 1], row, to
        )

    def block(level, slot, ch):
        return stores[level].at[slot, CHUNK[ch], :]

    def b_copy(level, ch, half, d):
        ref = block(level, 2 * x + half, ch)
        return send(ref, ref, b_send.at[level, ch, d], b_recv.at[level, ch, half], rows_of(x, (z + d) % NZ, core), col)

    def e_copy(level, ch, half, d):
        ref = block(level, 2 * across + half, ch)
        return send(ref, ref, e_send.at[level, ch, d], e_recv.at[level, ch, half], rows_of(x, (z + d) % NZ, core), col)

    def x_copy(level, ch, from_x):
        ref = block(level, 2 * from_x + own_half, ch)
        return send(ref, ref, x_send.at[level, ch], x_recv.at[level, ch], rows_of(across, z, core), col)

    def c_copy(level, ch, from_x, half, d):
        ref = block(level, 2 * from_x + half, ch)
        i = (d - 1) // 2
        to = rows_of((x + d) % NX, z, core)
        return send(ref, ref, c_send.at[level, ch, half, i], c_recv.at[level, ch, half, i], to, col)

    def d_copy(level, ch, slot):
        ref = block(level, slot, ch)
        return send(ref, ref, d_send.at[level, ch, slot], d_recv.at[level, ch, slot], rows_of(x, z, 1 - core), col)

    def beside(level, ch, half):
        for d in (1, 3):
            c_copy(level, ch, x, half, d).start()

    def launch(level, ch):
        x_copy(level, ch, x).start()
        for d in FAR8:
            b_copy(level, ch, own_half, d).start()
        d_copy(level, ch, own_slot).start()

    def spread(level):
        other = 1 - own_half

        @pl.when(is_root)
        def _():
            for ch in range(NCH):
                x_copy(level, ch, across).wait_recv()
                for d in FAR8:
                    e_copy(level, ch, own_half, d).start()
                beside(level, ch, own_half)
                d_copy(level, ch, 2 * across + own_half).start()
            if level > 0:
                for d in FAR8:
                    o_copy(level, d).start()
            for ch in range(NCH):
                b_copy(level, ch, other, 1).wait_recv()
                beside(level, ch, other)
                d_copy(level, ch, 2 * x + other).start()
            for ch in range(NCH):
                e_copy(level, ch, other, 1).wait_recv()
                d_copy(level, ch, 2 * across + other).start()

        @pl.when(jnp.logical_and(in_lane, not_root))
        def _():
            for ch in range(NCH):
                for half in range(2):
                    b_copy(level, ch, half, 1).wait_recv()
                    beside(level, ch, half)
                    d_copy(level, ch, 2 * x + half).start()
            for ch in range(NCH):
                for half in range(2):
                    e_copy(level, ch, half, 1).wait_recv()
                    d_copy(level, ch, 2 * across + half).start()

        @pl.when(in_lane)
        def _():
            for ch in range(NCH):
                for half in range(2):
                    for d in (1, 3):
                        from_x = (x + NX - d) % NX
                        c_copy(level, ch, from_x, half, d).wait_recv()
                        d_copy(level, ch, 2 * from_x + half).start()

        @pl.when(jnp.logical_not(in_lane))
        def _():
            for ch in range(NCH):
                for slot in range(8):
                    d_copy(level, ch, slot).wait_recv()

    def drain(level):
        if level == LEV - 1:
            for d in FAR8:
                l_copy(d).wait_send()
            return
        if level > 0:

            @pl.when(not_root)
            def _():
                for ch in range(NCH):
                    r_copy(level, ch, 1).wait_send()

        @pl.when(is_root)
        def _():
            if level > 0:
                for d in FAR8:
                    o_copy(level, d).wait_send()
            for ch in range(NCH):
                x_copy(level, ch, x).wait_send()
                for d in FAR8:
                    b_copy(level, ch, own_half, d).wait_send()
                    e_copy(level, ch, own_half, d).wait_send()

        @pl.when(in_lane)
        def _():
            for ch in range(NCH):
                for half in range(2):
                    for d in (1, 3):
                        c_copy(level, ch, x, half, d).wait_send()
                for slot in range(8):
                    d_copy(level, ch, slot).wait_send()

    loads[0].wait()
    loads[1].wait()

    @pl.when(is_root)
    def _():
        whole = jnp.dot(rhs_full[0].astype(jnp.bfloat16), diag[0], preferred_element_type=jnp.float32)
        store0[own_slot] = whole.astype(jnp.bfloat16)

    loads[2].wait()
    out_ref[0] = jnp.dot(rhs_own[0].astype(jnp.bfloat16), diag[0], preferred_element_type=jnp.float32)
    pl.semaphore_wait(barrier, 2 * (NY - 1) + NX)

    @pl.when(is_root)
    def _():
        for ch in range(NCH):
            launch(0, ch)

    for copy in loads[3:]:
        copy.wait()
    spread(0)

    for level in range(1, LEV):
        live = counts_ref[level - 1]
        total = jnp.zeros((RHS, W), jnp.float32)
        for k in range(BPD):
            source = ids_ref[level - 1, 0, 0, k]
            place = (source % (NX * NZ * NC)) // NY
            held = source // (NX * NZ * NC)
            chosen = store0[place]
            for m in range(1, level):
                chosen = lax.select(held == m, stores[m][place], chosen)
            chosen = lax.select(k < live, chosen, jnp.zeros_like(chosen))
            total = total + jnp.dot(chosen, fac[level - 1, k], preferred_element_type=jnp.float32)
        part[...] = total
        part16[level - 1] = total.astype(jnp.bfloat16)
        if level == LEV - 1:
            break

        @pl.when(not_root)
        def _():
            d = (col + NY - root) % NY
            for ch in range(NCH):
                r_copy(level, ch, d).start()

        @pl.when(is_root)
        def _():
            for ch in range(NCH):
                update = part[CHUNK[ch], :]
                for d in (1, 7, 2, 6, 3, 5, 4):
                    r_copy(level, ch, d).wait_recv()
                    update = update + landed[level - 1, d, CHUNK[ch], :].astype(jnp.float32)
                reduced = (rhs_full[level, CHUNK[ch], :] - update).astype(jnp.bfloat16)
                solved = jnp.dot(reduced, diag[level], preferred_element_type=jnp.float32)
                stores[level][own_slot, CHUNK[ch], :] = solved.astype(jnp.bfloat16)
                solbuf[level - 1, CHUNK[ch], :] = solved
                launch(level, ch)

        spread(level)

    for d in FAR8:
        l_copy(d).start()
    for level in range(1, LEV - 1):

        @pl.when(is_root)
        def _():
            out_ref[level] = solbuf[level - 1, share(col), :]

        @pl.when(not_root)
        def _():
            o_copy(level, 1).wait_recv()
            out_ref[level] = obuf[level - 1]

    for level in range(LEV - 1):
        drain(level)
    update = part[share(col), :]
    for d in (1, 7, 2, 6, 3, 5, 4):
        l_copy(d).wait_recv()
        update = update + last[d].astype(jnp.float32)
    reduced = (rhs_own[LEV - 1] - update).astype(jnp.bfloat16)
    out_ref[LEV - 1] = jnp.dot(reduced, diag[LEV - 1], preferred_element_type=jnp.float32)
    drain(LEV - 1)


def shards(right_sides, factor_blocks, diag_inverses, source_ids, block_counts):
    dma = pltpu.SemaphoreType.DMA
    hbm = pl.BlockSpec(memory_space=pl.ANY)
    smem = pl.BlockSpec(memory_space=pltpu.SMEM)
    store = pltpu.VMEM((8, RHS, W), jnp.bfloat16)
    mid, spreads = LEV - 2, LEV - 1
    out = pl.pallas_call(
        kernel,
        out_shape=jax.ShapeDtypeStruct((LEV, SHARE, W), jnp.float32),
        in_specs=[smem, smem, hbm, hbm, hbm],
        out_specs=pl.BlockSpec(memory_space=pltpu.VMEM),
        scratch_shapes=[
            store, store, store,
            pltpu.VMEM((RHS, W), jnp.float32),
            pltpu.VMEM((LEV - 1, RHS, W), jnp.bfloat16),
            pltpu.VMEM((mid, NY, RHS, W), jnp.bfloat16),
            pltpu.VMEM((NY, SHARE, W), jnp.bfloat16),
            pltpu.VMEM((mid, RHS, W), jnp.float32),
            pltpu.VMEM((mid, SHARE, W), jnp.float32),
            pltpu.VMEM((LEV - 1, RHS, W), jnp.float32),
            pltpu.VMEM((LEV, SHARE, W), jnp.float32),
            pltpu.VMEM((LEV - 1, BPD, W, W), jnp.bfloat16),
            pltpu.VMEM((LEV, W, W), jnp.bfloat16),
            dma((3 * LEV,)),
            dma((mid, NCH)), dma((mid, NCH, NY)),
            dma((NY,)), dma((NY,)),
            dma((mid, NY)), dma((mid,)),
            dma((spreads, NCH, NZ)), dma((spreads, NCH, 2)),
            dma((spreads, NCH, NZ)), dma((spreads, NCH, 2)),
            dma((spreads, NCH)), dma((spreads, NCH)),
            dma((spreads, NCH, 2, 2)), dma((spreads, NCH, 2, 2)),
            dma((spreads, NCH, 8)), dma((spreads, NCH, 8)),
        ],
        compiler_params=pltpu.CompilerParams(collective_id=0, has_side_effects=True),
        name="levels",
    )(source_ids, block_counts.reshape(LEV - 1), right_sides, factor_blocks, diag_inverses)
    return out[:, None]


def solution(mesh):
    return jax.shard_map(
        shards,
        mesh=mesh,
        in_specs=(
            P(None, "rows", None, None),
            P(None, "rows", "cols", None, None, None),
            P(None, "rows", None, None),
            P(None, "rows", "cols", None),
            P(None, "rows", "cols"),
        ),
        out_specs=P(None, "rows", "cols", None),
        check_vma=False,
    )
```

```python
import jax
import jax.numpy as jnp
from jax import lax
from jax.experimental import pallas as pl
from jax.experimental.pallas import tpu as pltpu
from jax.sharding import PartitionSpec as P

LEV, NX, NZ, NC, NY = 4, 4, 8, 2, 8
W, RHS, BPD = 256, 128, 8
SHARE = RHS // NY
FAR8 = (5, 3, 6, 2, 7, 1, 4)
FAR4 = (2, 1, 3)
NCH = 1
CHUNK = [pl.ds(i * (RHS // NCH), RHS // NCH) for i in range(NCH)]
MESH = pl.DeviceIdType.MESH


def kernel(
    ids_ref, counts_ref, rhs_hbm, fac_hbm, diag_hbm, out_ref,
    store0, store1, store2, part, part16, landed, last, solbuf, obuf, rhs_full, rhs_own, fac, diag,
    load_sem, r_send, r_recv, l_send, l_recv, o_send, o_recv,
    b_send, b_recv, e_send, e_recv, x_send, x_recv, c_send, c_recv, d_send, d_recv,
):
    stores = (store0, store1, store2)
    row = lax.axis_index("rows")
    col = lax.axis_index("cols")
    x = row // (NZ * NC)
    z = (row // NC) % NZ
    core = row % NC
    root = row % NY
    src_core = col % NC
    in_lane = core == src_core
    is_root = root == col
    not_root = jnp.logical_not(is_root)
    own_half = z // (NZ // 2)
    own_slot = 2 * x + own_half
    across = (x + NX // 2) % NX

    def rows_of(xx, zz, cc):
        return (xx * NZ + zz) * NC + cc

    def share(c):
        return pl.ds(pl.multiple_of(c * SHARE, SHARE), SHARE)

    def send(src, dst, send_sem, recv_sem, r, c):
        return pltpu.make_async_remote_copy(src, dst, send_sem, recv_sem, device_id=(r, c), device_id_type=MESH)

    loads = [
        pltpu.make_async_copy(rhs_hbm.at[0, 0], rhs_full.at[0], load_sem.at[0]),
        pltpu.make_async_copy(diag_hbm.at[0, 0], diag.at[0], load_sem.at[1]),
        pltpu.make_async_copy(rhs_hbm.at[:, 0, share(col), :], rhs_own, load_sem.at[2]),
    ]
    for level in range(1, LEV):
        loads.append(
            pltpu.make_async_copy(fac_hbm.at[level - 1, 0, 0], fac.at[level - 1], load_sem.at[1 + 2 * level])
        )
        loads.append(pltpu.make_async_copy(diag_hbm.at[level, 0], diag.at[level], load_sem.at[2 + 2 * level]))
    for level in range(1, LEV - 1):
        loads.append(
            pltpu.make_async_copy(rhs_hbm.at[level, 0], rhs_full.at[level], load_sem.at[2 + 2 * (LEV - 1) + level])
        )
    for copy in loads:
        copy.start()

    barrier = pltpu.get_barrier_semaphore()
    for d in FAR8:
        pl.semaphore_signal(barrier, device_id=(row, (col + d) % NY), device_id_type=MESH)
        pl.semaphore_signal(barrier, device_id=(rows_of(x, (z + d) % NZ, core), col), device_id_type=MESH)
    for d in FAR4:
        pl.semaphore_signal(barrier, device_id=(rows_of((x + d) % NX, z, core), col), device_id_type=MESH)
    pl.semaphore_signal(barrier, device_id=(rows_of(x, z, 1 - core), col), device_id_type=MESH)

    def l_copy(d):
        to = (col + d) % NY
        return send(part16.at[LEV - 2, share(to), :], last.at[d], l_send.at[d], l_recv.at[d], row, to)

    def r_copy(level, ch, d):
        return send(
            part16.at[level - 1, CHUNK[ch], :],
            landed.at[level - 1, d, CHUNK[ch], :],
            r_send.at[level - 1, ch],
            r_recv.at[level - 1, ch, d],
            row,
            root,
        )

    def o_copy(level, d):
        to = (col + d) % NY
        return send(
            solbuf.at[level - 1, share(to), :], obuf.at[level - 1], o_send.at[level - 1, d], o_recv.at[level - 1], row, to
        )

    def block(level, slot, ch):
        return stores[level].at[slot, CHUNK[ch], :]

    def b_copy(level, ch, half, d):
        ref = block(level, 2 * x + half, ch)
        return send(ref, ref, b_send.at[level, ch, d], b_recv.at[level, ch, half], rows_of(x, (z + d) % NZ, core), col)

    def e_copy(level, ch, half, d):
        ref = block(level, 2 * across + half, ch)
        return send(ref, ref, e_send.at[level, ch, d], e_recv.at[level, ch, half], rows_of(x, (z + d) % NZ, core), col)

    def x_copy(level, ch, from_x):
        ref = block(level, 2 * from_x + own_half, ch)
        return send(ref, ref, x_send.at[level, ch], x_recv.at[level, ch], rows_of(across, z, core), col)

    def c_copy(level, ch, from_x, half, d):
        ref = block(level, 2 * from_x + half, ch)
        i = (d - 1) // 2
        to = rows_of((x + d) % NX, z, core)
        return send(ref, ref, c_send.at[level, ch, half, i], c_recv.at[level, ch, half, i], to, col)

    def d_copy(level, ch, slot):
        ref = block(level, slot, ch)
        return send(ref, ref, d_send.at[level, ch, slot], d_recv.at[level, ch, slot], rows_of(x, z, 1 - core), col)

    def beside(level, ch, half):
        for d in (1, 3):
            c_copy(level, ch, x, half, d).start()

    def launch(level, ch):
        x_copy(level, ch, x).start()
        for d in FAR8:
            b_copy(level, ch, own_half, d).start()
        d_copy(level, ch, own_slot).start()

    def spread(level):
        other = 1 - own_half

        @pl.when(is_root)
        def _():
            for ch in range(NCH):
                x_copy(level, ch, across).wait_recv()
                for d in FAR8:
                    e_copy(level, ch, own_half, d).start()
                beside(level, ch, own_half)
                d_copy(level, ch, 2 * across + own_half).start()
            if level > 0:
                for d in FAR8:
                    o_copy(level, d).start()
            for ch in range(NCH):
                b_copy(level, ch, other, 1).wait_recv()
                beside(level, ch, other)
                d_copy(level, ch, 2 * x + other).start()
            for ch in range(NCH):
                e_copy(level, ch, other, 1).wait_recv()
                d_copy(level, ch, 2 * across + other).start()

        @pl.when(jnp.logical_and(in_lane, not_root))
        def _():
            for ch in range(NCH):
                for half in range(2):
                    b_copy(level, ch, half, 1).wait_recv()
                    beside(level, ch, half)
                    d_copy(level, ch, 2 * x + half).start()
            for ch in range(NCH):
                for half in range(2):
                    e_copy(level, ch, half, 1).wait_recv()
                    d_copy(level, ch, 2 * across + half).start()

        @pl.when(in_lane)
        def _():
            for ch in range(NCH):
                for half in range(2):
                    for d in (1, 3):
                        from_x = (x + NX - d) % NX
                        c_copy(level, ch, from_x, half, d).wait_recv()
                        d_copy(level, ch, 2 * from_x + half).start()

        @pl.when(jnp.logical_not(in_lane))
        def _():
            for ch in range(NCH):
                for slot in range(8):
                    d_copy(level, ch, slot).wait_recv()

    def drain(level):
        if level == LEV - 1:
            for d in FAR8:
                l_copy(d).wait_send()
            return
        if level > 0:

            @pl.when(not_root)
            def _():
                for ch in range(NCH):
                    r_copy(level, ch, 1).wait_send()

        @pl.when(is_root)
        def _():
            if level > 0:
                for d in FAR8:
                    o_copy(level, d).wait_send()
            for ch in range(NCH):
                x_copy(level, ch, x).wait_send()
                for d in FAR8:
                    b_copy(level, ch, own_half, d).wait_send()
                    e_copy(level, ch, own_half, d).wait_send()

        @pl.when(in_lane)
        def _():
            for ch in range(NCH):
                for half in range(2):
                    for d in (1, 3):
                        c_copy(level, ch, x, half, d).wait_send()
                for slot in range(8):
                    d_copy(level, ch, slot).wait_send()

    loads[0].wait()
    loads[1].wait()

    @pl.when(is_root)
    def _():
        whole = jnp.dot(rhs_full[0].astype(jnp.bfloat16), diag[0], preferred_element_type=jnp.float32)
        store0[own_slot] = whole.astype(jnp.bfloat16)

    loads[2].wait()
    out_ref[0] = jnp.dot(rhs_own[0].astype(jnp.bfloat16), diag[0], preferred_element_type=jnp.float32)
    pl.semaphore_wait(barrier, 2 * (NY - 1) + NX)

    @pl.when(is_root)
    def _():
        for ch in range(NCH):
            launch(0, ch)

    for copy in loads[3:]:
        copy.wait()
    spread(0)

    for level in range(1, LEV):
        live = counts_ref[level - 1]
        total = jnp.zeros((RHS, W), jnp.float32)
        for k in range(BPD):
            source = ids_ref[level - 1, 0, 0, k]
            place = (source % (NX * NZ * NC)) // NY
            held = source // (NX * NZ * NC)
            chosen = store0[place]
            for m in range(1, level):
                chosen = lax.select(held == m, stores[m][place], chosen)
            chosen = lax.select(k < live, chosen, jnp.zeros_like(chosen))
            total = total + jnp.dot(chosen, fac[level - 1, k], preferred_element_type=jnp.float32)
        part[...] = total
        part16[level - 1] = total.astype(jnp.bfloat16)
        if level == LEV - 1:
            break

        @pl.when(not_root)
        def _():
            d = (col + NY - root) % NY
            for ch in range(NCH):
                r_copy(level, ch, d).start()

        @pl.when(is_root)
        def _():
            for ch in range(NCH):
                update = part[CHUNK[ch], :]
                for d in (1, 7, 2, 6, 3, 5, 4):
                    r_copy(level, ch, d).wait_recv()
                    update = update + landed[level - 1, d, CHUNK[ch], :].astype(jnp.float32)
                reduced = (rhs_full[level, CHUNK[ch], :] - update).astype(jnp.bfloat16)
                solved = jnp.dot(reduced, diag[level], preferred_element_type=jnp.float32)
                stores[level][own_slot, CHUNK[ch], :] = solved.astype(jnp.bfloat16)
                solbuf[level - 1, CHUNK[ch], :] = solved
                launch(level, ch)

        drain(level - 1)
        spread(level)

    for d in FAR8:
        l_copy(d).start()
    for level in range(1, LEV - 1):

        @pl.when(is_root)
        def _():
            out_ref[level] = solbuf[level - 1, share(col), :]

        @pl.when(not_root)
        def _():
            o_copy(level, 1).wait_recv()
            out_ref[level] = obuf[level - 1]

    drain(LEV - 2)
    update = part[share(col), :]
    for d in (1, 7, 2, 6, 3, 5, 4):
        l_copy(d).wait_recv()
        update = update + last[d].astype(jnp.float32)
    reduced = (rhs_own[LEV - 1] - update).astype(jnp.bfloat16)
    out_ref[LEV - 1] = jnp.dot(reduced, diag[LEV - 1], preferred_element_type=jnp.float32)
    drain(LEV - 1)


def shards(right_sides, factor_blocks, diag_inverses, source_ids, block_counts):
    dma = pltpu.SemaphoreType.DMA
    hbm = pl.BlockSpec(memory_space=pl.ANY)
    smem = pl.BlockSpec(memory_space=pltpu.SMEM)
    store = pltpu.VMEM((8, RHS, W), jnp.bfloat16)
    mid, spreads = LEV - 2, LEV - 1
    out = pl.pallas_call(
        kernel,
        out_shape=jax.ShapeDtypeStruct((LEV, SHARE, W), jnp.float32),
        in_specs=[smem, smem, hbm, hbm, hbm],
        out_specs=pl.BlockSpec(memory_space=pltpu.VMEM),
        scratch_shapes=[
            store, store, store,
            pltpu.VMEM((RHS, W), jnp.float32),
            pltpu.VMEM((LEV - 1, RHS, W), jnp.bfloat16),
            pltpu.VMEM((mid, NY, RHS, W), jnp.bfloat16),
            pltpu.VMEM((NY, SHARE, W), jnp.bfloat16),
            pltpu.VMEM((mid, RHS, W), jnp.float32),
            pltpu.VMEM((mid, SHARE, W), jnp.float32),
            pltpu.VMEM((LEV - 1, RHS, W), jnp.float32),
            pltpu.VMEM((LEV, SHARE, W), jnp.float32),
            pltpu.VMEM((LEV - 1, BPD, W, W), jnp.bfloat16),
            pltpu.VMEM((LEV, W, W), jnp.bfloat16),
            dma((3 * LEV,)),
            dma((mid, NCH)), dma((mid, NCH, NY)),
            dma((NY,)), dma((NY,)),
            dma((mid, NY)), dma((mid,)),
            dma((spreads, NCH, NZ)), dma((spreads, NCH, 2)),
            dma((spreads, NCH, NZ)), dma((spreads, NCH, 2)),
            dma((spreads, NCH)), dma((spreads, NCH)),
            dma((spreads, NCH, 2, 2)), dma((spreads, NCH, 2, 2)),
            dma((spreads, NCH, 8)), dma((spreads, NCH, 8)),
        ],
        compiler_params=pltpu.CompilerParams(collective_id=0, has_side_effects=True),
        name="levels",
    )(source_ids, block_counts.reshape(LEV - 1), right_sides, factor_blocks, diag_inverses)
    return out[:, None]


def solution(mesh):
    return jax.shard_map(
        shards,
        mesh=mesh,
        in_specs=(
            P(None, "rows", None, None),
            P(None, "rows", "cols", None, None, None),
            P(None, "rows", None, None),
            P(None, "rows", "cols", None),
            P(None, "rows", "cols"),
        ),
        out_specs=P(None, "rows", "cols", None),
        check_vma=False,
    )
```

```python
import jax
import jax.numpy as jnp
from jax import lax
from jax.experimental import pallas as pl
from jax.experimental.pallas import tpu as pltpu
from jax.sharding import PartitionSpec as P

LEV, NX, NZ, NC, NY = 4, 4, 8, 2, 8
W, RHS, BPD = 256, 128, 8
SHARE = RHS // NY
FAR8 = (5, 3, 6, 2, 7, 1, 4)
FAR4 = (2, 1, 3)
NCH = 1
CHUNK = [pl.ds(i * (RHS // NCH), RHS // NCH) for i in range(NCH)]
MESH = pl.DeviceIdType.MESH


def kernel(
    ids_ref, counts_ref, rhs_hbm, fac_hbm, diag_hbm, out_ref,
    store0, store1, store2, part, part16, landed, last, solbuf, obuf, rhs_full, rhs_own, fac, diag,
    load_sem, r_send, r_recv, l_send, l_recv, o_send, o_recv,
    b_send, b_recv, e_send, e_recv, x_send, x_recv, c_send, c_recv, d_send, d_recv,
):
    stores = (store0, store1, store2)
    row = lax.axis_index("rows")
    col = lax.axis_index("cols")
    x = row // (NZ * NC)
    z = (row // NC) % NZ
    core = row % NC
    root = row % NY
    src_core = col % NC
    in_lane = core == src_core
    is_root = root == col
    not_root = jnp.logical_not(is_root)
    own_half = z // (NZ // 2)
    own_slot = 2 * x + own_half
    across = (x + NX // 2) % NX

    def rows_of(xx, zz, cc):
        return (xx * NZ + zz) * NC + cc

    def share(c):
        return pl.ds(pl.multiple_of(c * SHARE, SHARE), SHARE)

    def send(src, dst, send_sem, recv_sem, r, c):
        return pltpu.make_async_remote_copy(src, dst, send_sem, recv_sem, device_id=(r, c), device_id_type=MESH)

    loads = [
        pltpu.make_async_copy(rhs_hbm.at[0, 0], rhs_full.at[0], load_sem.at[0]),
        pltpu.make_async_copy(diag_hbm.at[0, 0], diag.at[0], load_sem.at[1]),
        pltpu.make_async_copy(rhs_hbm.at[:, 0, share(col), :], rhs_own, load_sem.at[2]),
    ]
    for level in range(1, LEV):
        loads.append(
            pltpu.make_async_copy(fac_hbm.at[level - 1, 0, 0], fac.at[level - 1], load_sem.at[1 + 2 * level])
        )
        loads.append(pltpu.make_async_copy(diag_hbm.at[level, 0], diag.at[level], load_sem.at[2 + 2 * level]))
    for level in range(1, LEV - 1):
        loads.append(
            pltpu.make_async_copy(rhs_hbm.at[level, 0], rhs_full.at[level], load_sem.at[2 + 2 * (LEV - 1) + level])
        )
    for copy in loads:
        copy.start()

    barrier = pltpu.get_barrier_semaphore()
    for d in FAR8:
        pl.semaphore_signal(barrier, device_id=(row, (col + d) % NY), device_id_type=MESH)
        pl.semaphore_signal(barrier, device_id=(rows_of(x, (z + d) % NZ, core), col), device_id_type=MESH)
    for d in FAR4:
        pl.semaphore_signal(barrier, device_id=(rows_of((x + d) % NX, z, core), col), device_id_type=MESH)
    pl.semaphore_signal(barrier, device_id=(rows_of(x, z, 1 - core), col), device_id_type=MESH)

    def l_copy(d):
        to = (col + d) % NY
        return send(part16.at[LEV - 2, share(to), :], last.at[d], l_send.at[d], l_recv.at[d], row, to)

    def r_copy(level, ch, d):
        return send(
            part16.at[level - 1, CHUNK[ch], :],
            landed.at[level - 1, d, CHUNK[ch], :],
            r_send.at[level - 1, ch],
            r_recv.at[level - 1, ch, d],
            row,
            root,
        )

    def o_copy(level, d):
        to = (col + d) % NY
        return send(
            solbuf.at[level - 1, share(to), :], obuf.at[level - 1], o_send.at[level - 1, d], o_recv.at[level - 1], row, to
        )

    def block(level, slot, ch):
        return stores[level].at[slot, CHUNK[ch], :]

    def b_copy(level, ch, half, d):
        ref = block(level, 2 * x + half, ch)
        return send(ref, ref, b_send.at[level, ch, d], b_recv.at[level, ch, half], rows_of(x, (z + d) % NZ, core), col)

    def e_copy(level, ch, half, d):
        ref = block(level, 2 * across + half, ch)
        return send(ref, ref, e_send.at[level, ch, d], e_recv.at[level, ch, half], rows_of(x, (z + d) % NZ, core), col)

    def x_copy(level, ch, from_x):
        ref = block(level, 2 * from_x + own_half, ch)
        return send(ref, ref, x_send.at[level, ch], x_recv.at[level, ch], rows_of(across, z, core), col)

    def c_copy(level, ch, from_x, half, d):
        ref = block(level, 2 * from_x + half, ch)
        i = (d - 1) // 2
        to = rows_of((x + d) % NX, z, core)
        return send(ref, ref, c_send.at[level, ch, half, i], c_recv.at[level, ch, half, i], to, col)

    def d_copy(level, ch, slot):
        ref = block(level, slot, ch)
        return send(ref, ref, d_send.at[level, ch, slot], d_recv.at[level, ch, slot], rows_of(x, z, 1 - core), col)

    def beside(level, ch, half):
        for d in (1, 3):
            c_copy(level, ch, x, half, d).start()

    def launch(level, ch):
        x_copy(level, ch, x).start()
        for d in FAR8:
            b_copy(level, ch, own_half, d).start()
        d_copy(level, ch, own_slot).start()

    def spread(level):
        other = 1 - own_half

        @pl.when(is_root)
        def _():
            for ch in range(NCH):
                x_copy(level, ch, across).wait_recv()
                for d in FAR8:
                    e_copy(level, ch, own_half, d).start()
                beside(level, ch, own_half)
                d_copy(level, ch, 2 * across + own_half).start()
            if level > 0:
                for d in FAR8:
                    o_copy(level, d).start()
            for ch in range(NCH):
                b_copy(level, ch, other, 1).wait_recv()
                beside(level, ch, other)
                d_copy(level, ch, 2 * x + other).start()

        @pl.when(jnp.logical_and(in_lane, not_root))
        def _():
            for ch in range(NCH):
                for half in range(2):
                    b_copy(level, ch, half, 1).wait_recv()
                    beside(level, ch, half)
                    d_copy(level, ch, 2 * x + half).start()

        @pl.when(in_lane)
        def _():
            for ch in range(NCH):
                for half in range(2):
                    for d in (1, 3):
                        from_x = (x + NX - d) % NX
                        c_copy(level, ch, from_x, half, d).wait_recv()
                        d_copy(level, ch, 2 * from_x + half).start()

        @pl.when(is_root)
        def _():
            for ch in range(NCH):
                e_copy(level, ch, other, 1).wait_recv()
                d_copy(level, ch, 2 * across + other).start()

        @pl.when(jnp.logical_and(in_lane, not_root))
        def _():
            for ch in range(NCH):
                for half in range(2):
                    e_copy(level, ch, half, 1).wait_recv()
                    d_copy(level, ch, 2 * across + half).start()

        @pl.when(jnp.logical_not(in_lane))
        def _():
            for ch in range(NCH):
                for slot in range(8):
                    d_copy(level, ch, slot).wait_recv()

    def drain(level):
        if level == LEV - 1:
            for d in FAR8:
                l_copy(d).wait_send()
            return
        if level > 0:

            @pl.when(not_root)
            def _():
                for ch in range(NCH):
                    r_copy(level, ch, 1).wait_send()

        @pl.when(is_root)
        def _():
            if level > 0:
                for d in FAR8:
                    o_copy(level, d).wait_send()
            for ch in range(NCH):
                x_copy(level, ch, x).wait_send()
                for d in FAR8:
                    b_copy(level, ch, own_half, d).wait_send()
                    e_copy(level, ch, own_half, d).wait_send()

        @pl.when(in_lane)
        def _():
            for ch in range(NCH):
                for half in range(2):
                    for d in (1, 3):
                        c_copy(level, ch, x, half, d).wait_send()
                for slot in range(8):
                    d_copy(level, ch, slot).wait_send()

    loads[0].wait()
    loads[1].wait()

    @pl.when(is_root)
    def _():
        whole = jnp.dot(rhs_full[0].astype(jnp.bfloat16), diag[0], preferred_element_type=jnp.float32)
        store0[own_slot] = whole.astype(jnp.bfloat16)

    loads[2].wait()
    out_ref[0] = jnp.dot(rhs_own[0].astype(jnp.bfloat16), diag[0], preferred_element_type=jnp.float32)
    pl.semaphore_wait(barrier, 2 * (NY - 1) + NX)

    @pl.when(is_root)
    def _():
        for ch in range(NCH):
            launch(0, ch)

    for copy in loads[3:]:
        copy.wait()
    spread(0)

    for level in range(1, LEV):
        live = counts_ref[level - 1]
        total = jnp.zeros((RHS, W), jnp.float32)
        for k in range(BPD):
            source = ids_ref[level - 1, 0, 0, k]
            place = (source % (NX * NZ * NC)) // NY
            held = source // (NX * NZ * NC)
            chosen = store0[place]
            for m in range(1, level):
                chosen = lax.select(held == m, stores[m][place], chosen)
            chosen = lax.select(k < live, chosen, jnp.zeros_like(chosen))
            total = total + jnp.dot(chosen, fac[level - 1, k], preferred_element_type=jnp.float32)
        part16[level - 1] = total.astype(jnp.bfloat16)
        if level == LEV - 1:
            for d in FAR8:
                l_copy(d).start()
        part[...] = total
        if level == LEV - 1:
            break

        @pl.when(not_root)
        def _():
            d = (col + NY - root) % NY
            for ch in range(NCH):
                r_copy(level, ch, d).start()

        @pl.when(is_root)
        def _():
            for ch in range(NCH):
                update = part[CHUNK[ch], :]
                for d in (1, 7, 2, 6, 3, 5, 4):
                    r_copy(level, ch, d).wait_recv()
                    update = update + landed[level - 1, d, CHUNK[ch], :].astype(jnp.float32)
                reduced = (rhs_full[level, CHUNK[ch], :] - update).astype(jnp.bfloat16)
                solved = jnp.dot(reduced, diag[level], preferred_element_type=jnp.float32)
                stores[level][own_slot, CHUNK[ch], :] = solved.astype(jnp.bfloat16)
                solbuf[level - 1, CHUNK[ch], :] = solved
                launch(level, ch)

        drain(level - 1)
        spread(level)

    for level in range(1, LEV - 1):

        @pl.when(is_root)
        def _():
            out_ref[level] = solbuf[level - 1, share(col), :]

        @pl.when(not_root)
        def _():
            o_copy(level, 1).wait_recv()
            out_ref[level] = obuf[level - 1]

    drain(LEV - 2)
    update = part[share(col), :]
    for d in (1, 7, 2, 6, 3, 5, 4):
        l_copy(d).wait_recv()
        update = update + last[d].astype(jnp.float32)
    reduced = (rhs_own[LEV - 1] - update).astype(jnp.bfloat16)
    out_ref[LEV - 1] = jnp.dot(reduced, diag[LEV - 1], preferred_element_type=jnp.float32)
    drain(LEV - 1)


def shards(right_sides, factor_blocks, diag_inverses, source_ids, block_counts):
    dma = pltpu.SemaphoreType.DMA
    hbm = pl.BlockSpec(memory_space=pl.ANY)
    smem = pl.BlockSpec(memory_space=pltpu.SMEM)
    store = pltpu.VMEM((8, RHS, W), jnp.bfloat16)
    mid, spreads = LEV - 2, LEV - 1
    out = pl.pallas_call(
        kernel,
        out_shape=jax.ShapeDtypeStruct((LEV, SHARE, W), jnp.float32),
        in_specs=[smem, smem, hbm, hbm, hbm],
        out_specs=pl.BlockSpec(memory_space=pltpu.VMEM),
        scratch_shapes=[
            store, store, store,
            pltpu.VMEM((RHS, W), jnp.float32),
            pltpu.VMEM((LEV - 1, RHS, W), jnp.bfloat16),
            pltpu.VMEM((mid, NY, RHS, W), jnp.bfloat16),
            pltpu.VMEM((NY, SHARE, W), jnp.bfloat16),
            pltpu.VMEM((mid, RHS, W), jnp.float32),
            pltpu.VMEM((mid, SHARE, W), jnp.float32),
            pltpu.VMEM((LEV - 1, RHS, W), jnp.float32),
            pltpu.VMEM((LEV, SHARE, W), jnp.float32),
            pltpu.VMEM((LEV - 1, BPD, W, W), jnp.bfloat16),
            pltpu.VMEM((LEV, W, W), jnp.bfloat16),
            dma((3 * LEV,)),
            dma((mid, NCH)), dma((mid, NCH, NY)),
            dma((NY,)), dma((NY,)),
            dma((mid, NY)), dma((mid,)),
            dma((spreads, NCH, NZ)), dma((spreads, NCH, 2)),
            dma((spreads, NCH, NZ)), dma((spreads, NCH, 2)),
            dma((spreads, NCH)), dma((spreads, NCH)),
            dma((spreads, NCH, 2, 2)), dma((spreads, NCH, 2, 2)),
            dma((spreads, NCH, 8)), dma((spreads, NCH, 8)),
        ],
        compiler_params=pltpu.CompilerParams(collective_id=0, has_side_effects=True),
        name="levels",
    )(source_ids, block_counts.reshape(LEV - 1), right_sides, factor_blocks, diag_inverses)
    return out[:, None]


def solution(mesh):
    return jax.shard_map(
        shards,
        mesh=mesh,
        in_specs=(
            P(None, "rows", None, None),
            P(None, "rows", "cols", None, None, None),
            P(None, "rows", None, None),
            P(None, "rows", "cols", None),
            P(None, "rows", "cols"),
        ),
        out_specs=P(None, "rows", "cols", None),
        check_vma=False,
    )
```
